32 devices in a mesh: macro: 4 (over y, x), micro: 8 (over z, core).
Axes of the slice: x: 2, y: 2, z: 4, core: 2. Of those that a mesh axis runs over, the one named last changes fastest.
Arguments:
- displacement: float32 [3, 8, 16, 256], P(None, 'macro', 'micro'), may hold values from -6 to 6
- load: float32 [3, 8, 16, 256], P(None, 'macro', 'micro'), may hold values from -6 to 6
- routes: int32 [4, 8, 1024, 1], P('macro', 'micro'), may hold values from 0 to 7; in each aligned block of 1024 rows (0 to 1023, 1024 to 2047, ..., all dimensions but the last counted through in order) at most 256 rows name the same one
- counts: int32 [4, 8, 1024], P('macro', 'micro'), may hold values from 1 to 4
- stiffness: bfloat16 [8, 512, 512], P('micro'), may hold values from -0.5 to 2.5, as said below
- precond: bfloat16 [8, 512, 512], P('micro'), may hold values from -0.5 to 2.5, as said below
- forcing: bfloat16 [8, 6, 512], P('micro'), may hold values from -2.5 to 2.5
- coupling: bfloat16 [8, 512, 6], P('micro'), may hold values from -0.25 to 0.25
- lame_first: float32 [8], P('micro'), may hold values from 0.5 to 2
- lame_shear: float32 [8], P('micro'), may hold values from 0.5 to 2
Outputs:
- increment: float32 [3, 8, 16, 256], P(None, 'macro', 'micro')
- residual: float32 [3, 8, 16, 256], P(None, 'macro', 'micro')
The draws below stay inside these ranges and needn't reach their ends.
Inputs may be any that keep to these rules, and one draw needn't show every extreme that they name: `routes`: among the points of one block (one device's points), no owner is named by more than 256 points, a bound that some block reaches. `stiffness`: Symmetric. `precond`: Symmetric.
All inputs are finite; a program needn't handle non-finite values.
Results may differ from the reference program's by a relative error of at most 0.002.
Values sent between devices are 32-bit elements; how exact they have to be, the bound alone decides.
A program may use at most 64 MiB of HBM per device.

```python
import math
import jax
import jax.numpy as jnp
import numpy as np
from jax import lax

CX = 2
CY = 2
MODES = 512
ITMAX = 4
ITERS = 5
P_DEV = 1024
CAP = 256
MODELS = 8
NX = 8
NY = 16
NZ = 256
N_MACRO = 4
N_MICRO = 8


def model_scale(key):
    return jnp.exp(jax.random.uniform(jax.random.fold_in(key, 7), (MODELS,), jnp.float32, math.log(0.7), math.log(1.4)))


def model_matrix(key, scale):
    gauss = jax.random.truncated_normal(key, -4.0, 4.0, (MODELS, MODES, MODES), jnp.float32) / jnp.sqrt(MODES * 1.0)
    symmetric = (gauss + jnp.swapaxes(gauss, 1, 2)) / 2.9
    identity = jnp.eye(MODES, dtype=jnp.float32)
    return scale[:, None, None] * (identity[None] + 0.45 * symmetric)


def draw_stiffness(key, part):
    scale = model_scale(key)
    return model_matrix(jax.random.fold_in(key, 11), scale).astype(jnp.bfloat16)


def draw_precond(key, part):
    scale = model_scale(key)
    return model_matrix(jax.random.fold_in(key, 13), 1.0 / scale).astype(jnp.bfloat16)


def plant(values, stream_key, least, top_value):
    shape = values.shape
    spot = [jax.random.randint(jax.random.fold_in(stream_key, axis), (), 0, shape[axis]) for axis in range(len(shape))]
    values = values.at[tuple(spot)].set(least)
    longest = shape.index(max(shape))
    spot[longest] = (spot[longest] + 1) % shape[longest]
    return values.at[tuple(spot)].set(top_value)


def block_levels(key, shape, pieces, smallest, largest):
    def one(axis_at, shards_of):
        heights = jax.random.uniform(jax.random.fold_in(jax.random.fold_in(key, 6), axis_at), (shards_of,), jnp.float32, smallest / len(pieces), largest / len(pieces))
        return jnp.repeat(jnp.exp(heights), shape[axis_at] // shards_of).reshape((-1,) + (1,) * (len(shape) - axis_at - 1))

    loudness = one(*pieces[0])
    for cut in pieces[1:]:
        loudness = loudness * one(*cut)
    return loudness


def deal_out(key, own, number, rows, amount, top, reach, lean):
    sequence = jax.random.permutation(key, amount)
    packed, common = shares(amount, rows * top, reach, lean, True), shares(amount, rows * top, reach, lean, False)
    places = jnp.arange(amount)

    def named(sizes, rotation):
        used = int((sizes > 0).sum())
        fixed = max(1, used // 4)
        shifted = fixed + (places - fixed + rotation * (used - fixed)) % max(1, amount - fixed)
        return jnp.zeros((amount,), jnp.int32).at[sequence[jnp.where(places < fixed, places, shifted)]].set(jnp.asarray(sizes, jnp.int32))

    sizes = jnp.where(number % 4 == 0, named(packed, number // 4), named(common, number - number // 4 - 1))
    mixed = jax.random.permutation(jax.random.fold_in(own, 3), amount)
    source_of, taker = mixed[0:amount // 2 * 2:2], mixed[1:amount // 2 * 2:2]
    room = jnp.minimum(sizes[source_of] - 1, reach - sizes[taker]) // 2
    room = jnp.where((source_of == sequence[0]) | (taker == sequence[0]) | (sizes[taker] == 0), 0, jnp.maximum(room, 0))
    shifted = jax.random.randint(jax.random.fold_in(own, 4), (amount // 2,), 0, 1 << 20) % (room + 1)
    sizes = sizes.at[source_of].add(-shifted).at[taker].add(shifted)
    members = jnp.searchsorted(jnp.cumsum(sizes), jnp.arange(rows * top), side="right").astype(jnp.int32)
    table = members.reshape(top, rows).T
    table = table[jax.random.permutation(jax.random.fold_in(own, 1), rows)]
    rotation = jax.random.randint(jax.random.fold_in(own, 2), (rows, 1), 0, top)
    return jnp.take_along_axis(table, (jnp.arange(top)[None, :] + rotation) % top, axis=1)


def shares(amount, total, reach, lean, full):
    loads = [(1 << 20) // math.isqrt(grade ** lean) + 1 for grade in range(1, amount + 1)]
    largest = reach if full else min(reach, max(-(-total // amount), total * loads[0] // sum(loads)))
    least = 1 if total - largest >= amount - 1 else 0
    holding, spare = [largest] + [least] * (amount - 1), total - largest - least * (amount - 1)
    while spare > 0:
        candidates = [i for i in range(1, amount) if holding[i] < largest] or [i for i in range(1, amount) if holding[i] < reach]
        whole, budget = sum([loads[i] for i in candidates]), spare
        for i in candidates:
            more = min(reach - holding[i], max(1, budget * loads[i] // whole), spare)
            holding[i] = holding[i] + more
            spare = spare - more
    return np.array(holding)


def normal_values(key, dims, spread, reach, cuts=(), held_as=jnp.bfloat16):
    values = jax.random.normal(key, dims, jnp.float32) * spread
    if len(cuts) > 0:
        values = block_levels(key, dims, cuts, -0.22, 0.18) * values
    return jnp.clip(values, min=-reach, max=reach).astype(held_as)


def setup_inputs(seed: int = 0) -> dict:
    keys = jax.random.split(jax.random.key(seed), 11)
    displacement = normal_values(keys[0], (3, NX, NY, NZ), 1.0, 6.0, ((1, 4), (2, 8)), jnp.float32)
    load = normal_values(keys[1], (3, NX, NY, NZ), 1.0, 6.0, ((1, 4), (2, 8)), jnp.float32)
    routes_keys = jax.random.split(jax.random.fold_in(keys[2], 1), N_MACRO * N_MICRO * P_DEV // P_DEV)
    routes_turns = jax.random.permutation(jax.random.fold_in(keys[2], 3), N_MACRO * N_MICRO * P_DEV // P_DEV)
    routes = jax.vmap(lambda own, number: deal_out(jax.random.fold_in(keys[2], 2), own, number, P_DEV, N_MICRO, 1, CAP, 2))(routes_keys, routes_turns).reshape((N_MACRO, N_MICRO, P_DEV, 1))
    counts = plant(jax.random.randint(keys[3], (N_MACRO, N_MICRO, P_DEV), 1, ITMAX + 1), jax.random.fold_in(keys[3], 1), 1, ITMAX).astype(jnp.int32)
    stiffness = draw_stiffness(jax.random.fold_in(keys[10], 71), 0)
    precond = draw_precond(jax.random.fold_in(keys[10], 71), 0)
    forcing = normal_values(keys[6], (MODELS, 6, MODES), 6 ** -0.5, 2.5, ((0, 8),))
    coupling = normal_values(keys[7], (MODELS, MODES, 6), MODES ** -0.5, 0.25, ((0, 8),))
    lame_first = jnp.clip(jnp.exp(math.log(2.0) - 1.3862944 * jax.random.uniform(keys[8], (MODELS,), jnp.float32) ** block_levels(keys[8], (MODELS,), ((0, 8),), -0.2, 0.2)), 0.5, 2.0)
    lame_shear = jnp.clip(jnp.exp(math.log(2.0) - 1.3862944 * jax.random.uniform(keys[9], (MODELS,), jnp.float32) ** block_levels(keys[9], (MODELS,), ((0, 8),), -0.2, 0.2)), 0.5, 2.0)
    return {"displacement": displacement, "load": load, "routes": routes, "counts": counts, "stiffness": stiffness, "precond": precond, "forcing": forcing, "coupling": coupling, "lame_first": lame_first, "lame_shear": lame_shear}


BETA = 0.1
OMEGA = 0.8
MASS = 0.1
VOIGT = ((0, 5, 4), (5, 1, 3), (4, 3, 2))
ALL_PAIRS = tuple((first_axis, second_axis) for first_axis in range(6) for second_axis in range(6))


def element_strain(nodes):
    count_x = nodes.shape[1] - 1
    count_y = nodes.shape[2] - 1
    count_z = nodes.shape[3]
    padded = jnp.pad(nodes, ((0, 0), (0, 0), (0, 0), (0, 1)))
    zeros = jnp.zeros((3, count_x, count_y, count_z), jnp.float32)
    grad_x, grad_y, grad_z = zeros, zeros, zeros
    for corner_x in (0, 1):
        for corner_y in (0, 1):
            for corner_z in (0, 1):
                piece = padded[:, corner_x:corner_x + count_x, corner_y:corner_y + count_y, corner_z:corner_z + count_z]
                grad_x = grad_x + (0.25 * (2 * corner_x - 1)) * piece
                grad_y = grad_y + (0.25 * (2 * corner_y - 1)) * piece
                grad_z = grad_z + (0.25 * (2 * corner_z - 1)) * piece
    return jnp.stack([grad_x[0], grad_y[1], grad_z[2], grad_z[1] + grad_y[2], grad_z[0] + grad_x[2], grad_y[0] + grad_x[1]])


def node_force(stress):
    count_x, count_y, count_z = stress.shape[1], stress.shape[2], stress.shape[3]
    forces = jnp.zeros((3, count_x + 1, count_y + 1, count_z + 1), jnp.float32)
    for corner_x in (0, 1):
        for corner_y in (0, 1):
            for corner_z in (0, 1):
                signs = (2 * corner_x - 1, 2 * corner_y - 1, 2 * corner_z - 1)
                parts = []
                for component in range(3):
                    table = VOIGT[component]
                    parts.append(0.25 * (signs[0] * stress[table[0]] + signs[1] * stress[table[1]] + signs[2] * stress[table[2]]))
                contrib = jnp.stack(parts)
                forces = forces + jnp.pad(contrib, ((0, 0), (corner_x, 1 - corner_x), (corner_y, 1 - corner_y), (corner_z, 1 - corner_z)))
    return forces


def micro_solve(strain, sweeps, stiffness, precond, forcing, coupling, lame_first, lame_shear, pairs):
    strain_half = strain.astype(jnp.bfloat16)
    modal_load = lax.dot_general(strain_half, forcing, (((0,), (0,)), ((), ())), preferred_element_type=jnp.float32)
    modes = jnp.zeros_like(modal_load)
    for sweep in range(ITMAX):
        misfit = jnp.dot(modes.astype(jnp.bfloat16), stiffness, preferred_element_type=jnp.float32) + BETA * jnp.tanh(modes) - modal_load
        update = modes - OMEGA * jnp.dot(misfit.astype(jnp.bfloat16), precond, preferred_element_type=jnp.float32)
        modes = jnp.where((sweeps[0] > sweep)[:, None], update, modes)
    trace = strain[0] + strain[1] + strain[2]
    elastic = jnp.stack([lame_first * trace + 2.0 * lame_shear * strain[0], lame_first * trace + 2.0 * lame_shear * strain[1], lame_first * trace + 2.0 * lame_shear * strain[2], lame_shear * strain[3], lame_shear * strain[4], lame_shear * strain[5]])
    stress = elastic + lax.dot_general(coupling, modes.astype(jnp.bfloat16), (((0,), (1,)), ((), ())), preferred_element_type=jnp.float32)
    slope = 1.0 - jnp.tanh(modes) ** 2
    wide = coupling.astype(jnp.float32)
    products = jnp.stack([wide[:, pair[0]] * wide[:, pair[1]] for pair in pairs], axis=1)
    extra = lax.dot_general(products, slope, (((0,), (1,)), ((), ())), precision=lax.Precision.HIGHEST, preferred_element_type=jnp.float32)
    base = jnp.stack([lame_first * float(pair[0] < 3 and pair[1] < 3) + lame_shear * (2.0 * float(pair[0] == pair[1] and pair[0] < 3) + float(pair[0] == pair[1] and pair[0] >= 3)) for pair in pairs])
    return jnp.concatenate([stress, extra + base[:, None]], axis=0)


def operate(field, tangent):
    padded = jnp.pad(field, ((0, 0), (0, 1), (0, 1), (0, 0)))
    strain = element_strain(padded)
    stress = jnp.sum(tangent * strain[None], axis=1)
    return MASS * field + node_force(stress)[:, :-1, :-1, :-1]


def reference(displacement, load, routes, counts, stiffness, precond, forcing, coupling, lame_first, lame_shear):
    strain_all = element_strain(jnp.pad(displacement, ((0, 0), (0, 1), (0, 1), (0, 0))))
    points = strain_all.reshape(6, N_MACRO, CX, N_MICRO, CY, NZ).transpose(0, 1, 3, 2, 4, 5).reshape(6, N_MACRO, N_MICRO, P_DEV)
    owner_of = routes[..., 0]
    onehot = (owner_of[..., None] == jnp.arange(N_MICRO, dtype=jnp.int32)).astype(jnp.int32)
    ranks = jnp.sum((jnp.cumsum(onehot, axis=2) - 1) * onehot, axis=-1)
    target = (owner_of * CAP + ranks).astype(jnp.int32)
    macro_index = jnp.arange(N_MACRO, dtype=jnp.int32)[:, None, None]
    source_index = jnp.arange(N_MICRO, dtype=jnp.int32)[None, :, None]
    strain_buffer = jnp.zeros((6, N_MACRO, N_MICRO, N_MICRO * CAP), jnp.float32).at[:, macro_index, source_index, target].set(points)
    sweep_buffer = jnp.zeros((N_MACRO, N_MICRO, N_MICRO * CAP), jnp.int32).at[macro_index, source_index, target].set(counts)
    strain_owner = strain_buffer.reshape(6, N_MACRO, N_MICRO, N_MICRO, CAP).transpose(3, 0, 1, 2, 4).reshape(N_MICRO, 6, N_MACRO * N_MICRO * CAP)
    sweep_owner = sweep_buffer.reshape(N_MACRO, N_MICRO, N_MICRO, CAP).transpose(2, 0, 1, 3).reshape(N_MICRO, 1, N_MACRO * N_MICRO * CAP)

    def solve_owner(bundle):
        return micro_solve(bundle[0], bundle[1], bundle[2], bundle[3], bundle[4], bundle[5], bundle[6], bundle[7], ALL_PAIRS)

    results = lax.map(solve_owner, (strain_owner, sweep_owner, stiffness, precond, forcing, coupling, lame_first, lame_shear))
    back = results.reshape(N_MICRO, 42, N_MACRO, N_MICRO, CAP).transpose(1, 2, 3, 0, 4).reshape(42, N_MACRO, N_MICRO, N_MICRO * CAP)
    picked = jnp.take_along_axis(back, target[None], axis=3)
    values = picked.reshape(42, N_MACRO, N_MICRO, CX, CY, NZ).transpose(0, 1, 3, 2, 4, 5).reshape(42, NX, NY, NZ)
    stress = values[:6]
    tangent = values[6:].reshape(6, 6, NX, NY, NZ)
    rhs = load - node_force(stress)[:, :-1, :-1, :-1]
    increment = jnp.zeros_like(rhs)
    residual, direction = rhs, rhs
    norm_now = jnp.sum(residual * residual)
    for step in range(ITERS):
        image = operate(direction, tangent)
        alpha = norm_now / jnp.sum(direction * image)
        increment = increment + alpha * direction
        residual = residual - alpha * image
        norm_next = jnp.sum(residual * residual)
        direction = residual + (norm_next / norm_now) * direction
        norm_now = norm_next
    return increment, residual
```

```python
import jax
import jax.numpy as jnp
from jax import lax
from jax.experimental import pallas as pl
from jax.experimental.pallas import tpu as pltpu
from jax.sharding import PartitionSpec as P

ITMAX = 4
ITERS = 5


BETA = 0.1
OMEGA = 0.8
MASS = 0.1
VOIGT = ((0, 5, 4), (5, 1, 3), (4, 3, 2))
PAIRS = tuple((first, second) for first in range(6) for second in range(first, 6))
PAIR_AT = {pair: at for at, pair in enumerate(PAIRS)}
AROUND = tuple((dx, dy) for dx in (-1, 0, 1) for dy in (-1, 0, 1) if (dx, dy) != (0, 0))
MESH = pl.DeviceIdType.MESH


def with_halo(block, sides, width):
    for axis, dim in sides:
        count = lax.axis_size(axis)
        forward = [(i, i + 1) for i in range(count - 1)]
        backward = [(target, source) for source, target in forward]
        low = lax.ppermute(
            lax.slice_in_dim(block, block.shape[dim] - width, None, axis=dim), axis, forward
        )
        high = lax.ppermute(lax.slice_in_dim(block, 0, width, axis=dim), axis, backward)
        block = jnp.concatenate([low, block, high], axis=dim)
    return block


def passed_along(value, axis, steps):
    count = lax.axis_size(axis)
    initial, last = (max(0, -steps), min(count, count - steps))
    return lax.ppermute(value, axis, [(source, source + steps) for source in range(initial, last)])


def element_strain(nodes):
    count_x = nodes.shape[1] - 1
    count_y = nodes.shape[2] - 1
    count_z = nodes.shape[3]
    padded = jnp.pad(nodes, ((0, 0), (0, 0), (0, 0), (0, 1)))
    zeros = jnp.zeros((3, count_x, count_y, count_z), jnp.float32)
    grad_x, grad_y, grad_z = (zeros, zeros, zeros)
    for corner_x in (0, 1):
        for corner_y in (0, 1):
            for corner_z in (0, 1):
                piece = padded[
                    :,
                    corner_x : corner_x + count_x,
                    corner_y : corner_y + count_y,
                    corner_z : corner_z + count_z,
                ]
                grad_x = grad_x + 0.25 * (2 * corner_x - 1) * piece
                grad_y = grad_y + 0.25 * (2 * corner_y - 1) * piece
                grad_z = grad_z + 0.25 * (2 * corner_z - 1) * piece
    return jnp.stack(
        [
            grad_x[0],
            grad_y[1],
            grad_z[2],
            grad_z[1] + grad_y[2],
            grad_z[0] + grad_x[2],
            grad_y[0] + grad_x[1],
        ]
    )


def node_force(stress):
    count_x, count_y, count_z = (stress.shape[1], stress.shape[2], stress.shape[3])
    forces = jnp.zeros((3, count_x + 1, count_y + 1, count_z + 1), jnp.float32)
    for corner_x in (0, 1):
        for corner_y in (0, 1):
            for corner_z in (0, 1):
                signs = (2 * corner_x - 1, 2 * corner_y - 1, 2 * corner_z - 1)
                parts = []
                for component in range(3):
                    table = VOIGT[component]
                    parts.append(
                        0.25
                        * (
                            signs[0] * stress[table[0]]
                            + signs[1] * stress[table[1]]
                            + signs[2] * stress[table[2]]
                        )
                    )
                contrib = jnp.stack(parts)
                forces = forces + jnp.pad(
                    contrib,
                    (
                        (0, 0),
                        (corner_x, 1 - corner_x),
                        (corner_y, 1 - corner_y),
                        (corner_z, 1 - corner_z),
                    ),
                )
    return forces


def micro_solve(
    strain, sweeps, stiffness, precond, forcing, coupling, lame_first, lame_shear, pairs
):
    strain_half = strain.astype(jnp.bfloat16)
    modal_load = lax.dot_general(
        strain_half, forcing, (((0,), (0,)), ((), ())), preferred_element_type=jnp.float32
    )
    modes = jnp.zeros_like(modal_load)
    for sweep in range(ITMAX):
        misfit = (
            jnp.dot(modes.astype(jnp.bfloat16), stiffness, preferred_element_type=jnp.float32)
            + BETA * jnp.tanh(modes)
            - modal_load
        )
        update = modes - OMEGA * jnp.dot(
            misfit.astype(jnp.bfloat16), precond, preferred_element_type=jnp.float32
        )
        modes = jnp.where((sweeps[0] > sweep)[:, None], update, modes)
    trace = strain[0] + strain[1] + strain[2]
    elastic = jnp.stack(
        [
            lame_first * trace + 2.0 * lame_shear * strain[0],
            lame_first * trace + 2.0 * lame_shear * strain[1],
            lame_first * trace + 2.0 * lame_shear * strain[2],
            lame_shear * strain[3],
            lame_shear * strain[4],
            lame_shear * strain[5],
        ]
    )
    stress = elastic + lax.dot_general(
        coupling,
        modes.astype(jnp.bfloat16),
        (((0,), (1,)), ((), ())),
        preferred_element_type=jnp.float32,
    )
    slope = 1.0 - jnp.tanh(modes) ** 2
    wide = coupling.astype(jnp.float32)
    products = jnp.stack([wide[:, pair[0]] * wide[:, pair[1]] for pair in pairs], axis=1)
    extra = lax.dot_general(
        products.astype(jnp.bfloat16),
        slope.astype(jnp.bfloat16),
        (((0,), (1,)), ((), ())),
        preferred_element_type=jnp.float32,
    )
    base = jnp.stack(
        [
            lame_first * float(pair[0] < 3 and pair[1] < 3)
            + lame_shear
            * (
                2.0 * float(pair[0] == pair[1] and pair[0] < 3)
                + float(pair[0] == pair[1] and pair[0] >= 3)
            )
            for pair in pairs
        ]
    )
    return jnp.concatenate([stress, extra + base[:, None]], axis=0)


def extend(field):
    return with_halo(field, (("macro", 1), ("micro", 2)), 1)


def cg_kernel(
    sizes,
    load_ref,
    elem_ref,
    inc_ref,
    res_ref,
    residual,
    direction,
    along,
    increment,
    image,
    send_halo,
    halo,
    part,
    got_micro,
    middle,
    got_macro,
    send_sem,
    recv_sem,
    micro_send,
    micro_recv,
    macro_send,
    macro_recv,
):
    count_x, count_y, n_macro, n_micro = sizes
    wide = count_y + 2
    rows, lanes = load_ref.shape[1], load_ref.shape[2]
    a, b = lax.axis_index("macro"), lax.axis_index("micro")

    def inside(dx, dy):
        test = None
        for place, step, count in ((a, dx, n_macro), (b, dy, n_micro)):
            if step != 0:
                good = (place > 0) if step < 0 else (place < count - 1)
                test = good if test is None else jnp.logical_and(test, good)
        return test

    barrier = pltpu.get_barrier_semaphore()
    for step in range(1, n_micro):
        pl.semaphore_signal(
            barrier, inc=1, device_id=(a, lax.rem(b + step, n_micro)), device_id_type=MESH
        )
    for step in range(1, n_macro):
        pl.semaphore_signal(
            barrier, inc=1, device_id=(lax.rem(a + step, n_macro), b), device_id_type=MESH
        )
    corners = [(dx, dy) for dx, dy in AROUND if dx != 0 and dy != 0]
    for dx, dy in corners:
        pl.semaphore_signal(
            barrier,
            inc=1,
            device_id=(lax.rem(a + dx + n_macro, n_macro), lax.rem(b + dy + n_micro, n_micro)),
            device_id_type=MESH,
        )
    pl.semaphore_wait(barrier, n_micro - 1 + n_macro - 1 + len(corners))
    for at, (dx, dy) in enumerate(AROUND):

        @pl.when(jnp.logical_not(inside(dx, dy)))
        def _():
            for it in range(ITERS + 1):
                halo[it, at] = jnp.zeros(halo.shape[2:], jnp.float32)

    def near(step, count):
        return {0: list(range(1, count + 1)), -1: [1], 1: [count]}[step]

    def far(step, count):
        return {0: list(range(1, count + 1)), -1: [0], 1: [count + 1]}[step]

    def places(at, pick):
        dx, dy = AROUND[at]
        return [i * wide + j for i in pick(dx, count_x) for j in pick(dy, count_y)]

    def hop(it, at):
        dx, dy = AROUND[at]
        other = len(AROUND) - 1 - at
        return pltpu.make_async_remote_copy(
            src_ref=send_halo.at[it, at],
            dst_ref=halo.at[it, other],
            send_sem=send_sem.at[it, at],
            recv_sem=recv_sem.at[it, other],
            device_id=(a + dx, b + dy),
            device_id_type=MESH,
        )

    def halo_start(it, ref):
        for at, (dx, dy) in enumerate(AROUND):

            @pl.when(inside(dx, dy))
            def _():
                mine = places(at, near)
                for c in range(3):
                    for k, row in enumerate(mine):
                        send_halo[it, at, pl.ds(c * len(mine) + k, 1)] = ref[c, pl.ds(row, 1)]
                hop(it, at).start()

    def halo_finish(it, ref):
        for at, (dx, dy) in enumerate(AROUND):

            @pl.when(inside(dx, dy))
            def _():
                hop(it, at).wait_send()
                pltpu.make_async_remote_copy(
                    src_ref=send_halo.at[it, at],
                    dst_ref=halo.at[it, at],
                    send_sem=send_sem.at[it, at],
                    recv_sem=recv_sem.at[it, at],
                    device_id=(a + dx, b + dy),
                    device_id_type=MESH,
                ).wait_recv()

        for at in range(len(AROUND)):
            theirs = places(at, far)
            for c in range(3):
                for k, row in enumerate(theirs):
                    ref[c, pl.ds(row, 1)] = halo[it, at, pl.ds(c * len(theirs) + k, 1)]

    row_at = lax.broadcasted_iota(jnp.int32, (rows, lanes), 0)
    lane_at = lax.broadcasted_iota(jnp.int32, (rows, lanes), 1)
    own = row_at < 0
    for i in range(1, count_x + 1):
        low = i * wide + 1
        own = jnp.logical_or(own, jnp.logical_and(row_at >= low, row_at < low + count_y))

    def up(value, axis):
        if axis == 2:
            moved = pltpu.roll(value, lanes - 1, 1)
            return jnp.where(lane_at == lanes - 1, 0.0, moved)
        return pltpu.roll(value, rows - (wide if axis == 0 else 1), 0)

    def down(value, axis):
        if axis == 2:
            return jnp.where(lane_at == 0, 0.0, pltpu.roll(value, 1, 1))
        return pltpu.roll(value, wide if axis == 0 else 1, 0)

    def strain_of(ref):
        grads = []
        for c in range(3):
            value = ref[c]
            moved = up(value, 2)
            total, gap = value + moved, moved - value
            total_up, gap_up = up(total, 1), up(gap, 1)
            flat, slope_y, slope_z = total + total_up, total_up - total, gap + gap_up
            grads.append(
                (
                    0.25 * (up(flat, 0) - flat),
                    0.25 * (up(slope_y, 0) + slope_y),
                    0.25 * (up(slope_z, 0) + slope_z),
                )
            )
        return [
            grads[0][0],
            grads[1][1],
            grads[2][2],
            grads[1][2] + grads[2][1],
            grads[0][2] + grads[2][0],
            grads[0][1] + grads[1][0],
        ]

    def force_of(stress, c):
        first, second, third = (stress[VOIGT[c][d]] for d in range(3))
        first = first + down(first, 2)
        second = second + down(second, 2)
        third = down(third, 2) - third
        first = first + down(first, 1)
        rest = down(second, 1) - second + third + down(third, 1)
        return 0.25 * (down(first, 0) - first + rest + down(rest, 0))

    stress = [elem_ref[i] for i in range(6)]
    for c in range(3):
        residual[c] = jnp.where(own, load_ref[c] - force_of(stress, c), 0.0)
        direction[c] = jnp.zeros((rows, lanes), jnp.float32)
        along[c] = jnp.zeros((rows, lanes), jnp.float32)
        increment[c] = jnp.zeros((rows, lanes), jnp.float32)
    halo_start(ITERS, residual)
    halo_finish(ITERS, residual)

    def gather_start(it, src, dst, count, me, send, recv, device):
        copies = []
        for step in range(1, count):
            copy = pltpu.make_async_remote_copy(
                src_ref=src.at[it],
                dst_ref=dst.at[it, me],
                send_sem=send.at[it, step - 1],
                recv_sem=recv.at[it, step - 1],
                device_id=device(lax.rem(me + step, count)),
                device_id_type=MESH,
            )
            copy.start()
            copies.append(copy)
        dst[it, me] = src[it]
        return copies

    def gather_finish(it, copies, dst, count):
        for copy in copies:
            copy.wait()
        total = dst[it, 0]
        for at in range(1, count):
            total = total + dst[it, at]
        return total

    def step_body(it, carry):
        norm_old, alpha_old = carry
        strain = strain_of(residual)
        stress = []
        for i in range(6):
            value = None
            for j in range(6):
                term = elem_ref[6 + PAIR_AT[(min(i, j), max(i, j))]] * strain[j]
                value = term if value is None else value + term
            stress.append(value)
        norm = jnp.zeros((rows, lanes), jnp.float32)
        cross = jnp.zeros((rows, lanes), jnp.float32)
        for c in range(3):
            here = residual[c]
            new = jnp.where(own, MASS * here + force_of(stress, c), 0.0)
            image[c] = new
            kept = jnp.where(own, here, 0.0)
            norm = norm + kept * kept
            cross = cross + kept * new

        def folded(value):
            value = jnp.sum(value, axis=0, keepdims=True)
            total = value[:, :128]
            for at in range(128, lanes, 128):
                total = total + value[:, at : at + 128]
            return total

        tile_row = lax.broadcasted_iota(jnp.int32, (8, 128), 0)
        part[it] = jnp.where(
            tile_row == 0, folded(norm), jnp.where(tile_row == 1, folded(cross), 0.0)
        )
        copies = gather_start(
            it, part, got_micro, n_micro, b, micro_send, micro_recv, lambda other: (a, other)
        )
        halo_start(it, image)
        middle[it] = gather_finish(it, copies, got_micro, n_micro)
        copies = gather_start(
            it, middle, got_macro, n_macro, a, macro_send, macro_recv, lambda other: (other, b)
        )
        halo_finish(it, image)
        totals = jnp.sum(gather_finish(it, copies, got_macro, n_macro), axis=1, keepdims=True)
        norm_now, product = totals[0:1], totals[1:2]
        first = jnp.full((1, 1), it, jnp.int32) == 0
        ratio = jnp.where(first, 0.0, norm_now / norm_old)
        alpha = norm_now / (product - ratio * norm_now / alpha_old)
        for c in range(3):
            here = residual[c]
            toward = here + ratio * direction[c]
            drop = image[c] + ratio * along[c]
            direction[c] = toward
            along[c] = drop
            increment[c] = increment[c] + alpha * toward
            residual[c] = here - alpha * drop
        return norm_now, alpha

    lax.fori_loop(
        0, ITERS, step_body, (jnp.ones((1, 1), jnp.float32), jnp.ones((1, 1), jnp.float32))
    )
    for c in range(3):
        for i in range(count_x):
            low = (i + 1) * wide + 1
            inc_ref[c, i] = increment[c, pl.ds(low, count_y)]
            res_ref[c, i] = residual[c, pl.ds(low, count_y)]


def conjugate_gradients(load, elements):
    _, count_x, count_y, count_z = load.shape
    n_macro, n_micro = lax.axis_size("macro"), lax.axis_size("micro")
    flat = (count_x + 2) * (count_y + 2)
    rows = -(-flat // 8) * 8

    def laid(value, high):
        value = jnp.pad(value, ((0, 0), (1 - high, 1), (1 - high, 1), (0, 0)))
        value = value.reshape(value.shape[0], flat, count_z)
        return jnp.pad(value, ((0, 0), (0, rows - flat), (0, 0)))

    side = -(-3 * max(count_x, count_y) // 8) * 8
    node = pltpu.VMEM((3, rows, count_z), jnp.float32)
    around = pltpu.VMEM((ITERS + 1, len(AROUND), side, count_z), jnp.float32)
    dma = pltpu.SemaphoreType.DMA

    def body(*refs):
        cg_kernel((count_x, count_y, n_macro, n_micro), *refs)

    vmem = pl.BlockSpec(memory_space=pltpu.VMEM)
    return pl.pallas_call(
        body,
        out_shape=[jax.ShapeDtypeStruct(load.shape, jnp.float32)] * 2,
        in_specs=[vmem, vmem],
        out_specs=[vmem, vmem],
        scratch_shapes=[node] * 5
        + [
            around,
            around,
            pltpu.VMEM((ITERS, 8, 128), jnp.float32),
            pltpu.VMEM((ITERS, n_micro, 8, 128), jnp.float32),
            pltpu.VMEM((ITERS, 8, 128), jnp.float32),
            pltpu.VMEM((ITERS, n_macro, 8, 128), jnp.float32),
            dma((ITERS + 1, len(AROUND))),
            dma((ITERS + 1, len(AROUND))),
            dma((ITERS, n_micro - 1)),
            dma((ITERS, n_micro - 1)),
            dma((ITERS, n_macro - 1)),
            dma((ITERS, n_macro - 1)),
        ],
        compiler_params=pltpu.CompilerParams(collective_id=0, has_side_effects=True),
        name="conjugate_gradients",
    )(laid(load, 0), laid(elements, 1))


def shards(
    displacement,
    load,
    routes,
    counts,
    stiffness,
    precond,
    forcing,
    coupling,
    lame_first,
    lame_shear,
):
    count_x, count_y, count_z = (
        displacement.shape[1],
        displacement.shape[2],
        displacement.shape[3],
    )
    points = count_x * count_y * count_z
    owners = lax.axis_size("micro")
    capacity = max(2, 2 * points // owners)
    strain_ext = element_strain(extend(displacement))
    strain_points = strain_ext[:, 1:, 1:].reshape(6, points)
    owner_of = routes.reshape(points)
    sweeps_of = counts.reshape(points)
    onehot = (owner_of[:, None] == jnp.arange(owners, dtype=jnp.int32)[None, :]).astype(jnp.int32)
    ranks = jnp.sum((jnp.cumsum(onehot, axis=0) - 1) * onehot, axis=1)
    target = owner_of * capacity + ranks
    bundle = jnp.concatenate([strain_points, sweeps_of.astype(jnp.float32)[None]], axis=0)
    send = jnp.zeros((7, owners * capacity), jnp.float32).at[:, target].set(
        bundle, unique_indices=True, mode="promise_in_bounds"
    )
    got = lax.all_to_all(send, "micro", split_axis=1, concat_axis=1, tiled=True)
    got_strain, got_sweeps = got[:6], got[6:]
    rows = micro_solve(
        got_strain,
        got_sweeps,
        stiffness[0],
        precond[0],
        forcing[0],
        coupling[0],
        lame_first[0],
        lame_shear[0],
        PAIRS,
    )
    back = lax.all_to_all(rows, "micro", split_axis=1, concat_axis=1, tiled=True)
    values = jnp.take(back, target, axis=1, unique_indices=True, mode="clip")
    values = values.reshape(back.shape[0], count_x, count_y, count_z)
    left_x = passed_along(values[:, -1:], "macro", 1)
    values = jnp.concatenate([left_x, values], axis=1)
    left_y = passed_along(values[:, :, -1:], "micro", 1)
    values = jnp.concatenate([left_y, values], axis=2)
    return tuple(conjugate_gradients(load, values))


def solution(mesh):
    in_specs = (
        P(None, "macro", "micro", None),
        P(None, "macro", "micro", None),
        P("macro", "micro", None, None),
        P("macro", "micro", None),
        P("micro", None, None),
        P("micro", None, None),
        P("micro", None, None),
        P("micro", None, None),
        P("micro"),
        P("micro"),
    )
    out_specs = (P(None, "macro", "micro", None), P(None, "macro", "micro", None))
    return jax.shard_map(shards, mesh=mesh, in_specs=in_specs, out_specs=out_specs, check_vma=False)
```

```python
import jax
import jax.numpy as jnp
from jax import lax
from jax.experimental import pallas as pl
from jax.experimental.pallas import tpu as pltpu
from jax.sharding import PartitionSpec as P

ITMAX = 4
ITERS = 5


BETA = 0.1
OMEGA = 0.8
MASS = 0.1
VOIGT = ((0, 5, 4), (5, 1, 3), (4, 3, 2))
PAIRS = tuple((first, second) for first in range(6) for second in range(first, 6))
PAIR_AT = {pair: at for at, pair in enumerate(PAIRS)}
AROUND = tuple((dx, dy) for dx in (-1, 0, 1) for dy in (-1, 0, 1) if (dx, dy) != (0, 0))
MESH = pl.DeviceIdType.MESH


def with_halo(block, sides, width):
    for axis, dim in sides:
        count = lax.axis_size(axis)
        forward = [(i, i + 1) for i in range(count - 1)]
        backward = [(target, source) for source, target in forward]
        low = lax.ppermute(
            lax.slice_in_dim(block, block.shape[dim] - width, None, axis=dim), axis, forward
        )
        high = lax.ppermute(lax.slice_in_dim(block, 0, width, axis=dim), axis, backward)
        block = jnp.concatenate([low, block, high], axis=dim)
    return block


def passed_along(value, axis, steps):
    count = lax.axis_size(axis)
    initial, last = (max(0, -steps), min(count, count - steps))
    return lax.ppermute(value, axis, [(source, source + steps) for source in range(initial, last)])


def element_strain(nodes):
    count_x = nodes.shape[1] - 1
    count_y = nodes.shape[2] - 1
    count_z = nodes.shape[3]
    padded = jnp.pad(nodes, ((0, 0), (0, 0), (0, 0), (0, 1)))
    zeros = jnp.zeros((3, count_x, count_y, count_z), jnp.float32)
    grad_x, grad_y, grad_z = (zeros, zeros, zeros)
    for corner_x in (0, 1):
        for corner_y in (0, 1):
            for corner_z in (0, 1):
                piece = padded[
                    :,
                    corner_x : corner_x + count_x,
                    corner_y : corner_y + count_y,
                    corner_z : corner_z + count_z,
                ]
                grad_x = grad_x + 0.25 * (2 * corner_x - 1) * piece
                grad_y = grad_y + 0.25 * (2 * corner_y - 1) * piece
                grad_z = grad_z + 0.25 * (2 * corner_z - 1) * piece
    return jnp.stack(
        [
            grad_x[0],
            grad_y[1],
            grad_z[2],
            grad_z[1] + grad_y[2],
            grad_z[0] + grad_x[2],
            grad_y[0] + grad_x[1],
        ]
    )


def node_force(stress):
    count_x, count_y, count_z = (stress.shape[1], stress.shape[2], stress.shape[3])
    forces = jnp.zeros((3, count_x + 1, count_y + 1, count_z + 1), jnp.float32)
    for corner_x in (0, 1):
        for corner_y in (0, 1):
            for corner_z in (0, 1):
                signs = (2 * corner_x - 1, 2 * corner_y - 1, 2 * corner_z - 1)
                parts = []
                for component in range(3):
                    table = VOIGT[component]
                    parts.append(
                        0.25
                        * (
                            signs[0] * stress[table[0]]
                            + signs[1] * stress[table[1]]
                            + signs[2] * stress[table[2]]
                        )
                    )
                contrib = jnp.stack(parts)
                forces = forces + jnp.pad(
                    contrib,
                    (
                        (0, 0),
                        (corner_x, 1 - corner_x),
                        (corner_y, 1 - corner_y),
                        (corner_z, 1 - corner_z),
                    ),
                )
    return forces


def micro_kernel(bundle_ref, stiff_ref, pre_ref, force_ref, couple_ref, product_ref, coef_ref, out_ref):
    bundle = bundle_ref[...]
    sweeps = bundle[6:7]
    modal_load = jnp.dot(
        force_ref[...], bundle.astype(jnp.bfloat16), preferred_element_type=jnp.float32
    )
    modes = None
    for sweep in range(ITMAX):
        misfit = -modal_load
        if modes is not None:
            misfit = (
                jnp.dot(
                    stiff_ref[...], modes.astype(jnp.bfloat16), preferred_element_type=jnp.float32
                )
                + BETA * jnp.tanh(modes)
                - modal_load
            )
        change = OMEGA * jnp.dot(
            pre_ref[...], misfit.astype(jnp.bfloat16), preferred_element_type=jnp.float32
        )
        before = jnp.zeros_like(change) if modes is None else modes
        modes = jnp.where(sweeps > sweep, before - change, before)
    bent = jnp.tanh(modes)
    slope = 1.0 - bent * bent
    trace = bundle[0:1] + bundle[1:2] + bundle[2:3]
    rows = coef_ref.shape[0]
    tall = jnp.concatenate(
        [bundle, jnp.zeros((rows - bundle.shape[0], bundle.shape[1]), jnp.float32)], axis=0
    )
    coef = coef_ref[...]
    total = coef[:, 0:1] * trace + coef[:, 1:2] * tall + coef[:, 2:3]
    total = total + jnp.dot(
        couple_ref[...], modes.astype(jnp.bfloat16), preferred_element_type=jnp.float32
    )
    total = total + jnp.dot(
        product_ref[...], slope.astype(jnp.bfloat16), preferred_element_type=jnp.float32
    )
    out_ref[...] = total[: out_ref.shape[0]]


def micro_solve(bundle, stiffness, precond, forcing, coupling, lame_first, lame_shear, pairs):
    size, points = stiffness.shape[0], bundle.shape[1]
    tile = 512 if points % 512 == 0 else points
    count = 6 + len(pairs)
    rows = -(-count // 8) * 8
    force = jnp.pad(forcing.T, ((0, 0), (0, 2)))
    wide = coupling.astype(jnp.float32).T
    products = jnp.stack([wide[first] * wide[second] for first, second in pairs])
    products = jnp.pad(products.astype(jnp.bfloat16), ((6, rows - count), (0, 0)))
    couple = jnp.pad(coupling.T, ((0, rows - 6), (0, 0)))
    on_trace = jnp.array([1.0] * 3 + [0.0] * (rows - 3), jnp.float32)
    on_shear = jnp.array([2.0] * 3 + [1.0] * 3 + [0.0] * (rows - 6), jnp.float32)
    base_first = [0.0] * 6 + [float(i < 3 and j < 3) for i, j in pairs] + [0.0] * (rows - count)
    base_shear = (
        [0.0] * 6
        + [float(i == j) * (2.0 if i < 3 else 1.0) for i, j in pairs]
        + [0.0] * (rows - count)
    )
    base = lame_first * jnp.array(base_first, jnp.float32) + lame_shear * jnp.array(
        base_shear, jnp.float32
    )
    coef = jnp.stack([lame_first * on_trace, lame_shear * on_shear, base], axis=1)

    def whole(shape):
        return pl.BlockSpec(shape, lambda i: (0, 0))

    return pl.pallas_call(
        micro_kernel,
        grid=(points // tile,),
        out_shape=jax.ShapeDtypeStruct((count, points), jnp.float32),
        in_specs=[
            pl.BlockSpec((8, tile), lambda i: (0, i)),
            whole((size, size)),
            whole((size, size)),
            whole((size, 8)),
            whole((rows, size)),
            whole((rows, size)),
            whole((rows, 3)),
        ],
        out_specs=pl.BlockSpec((count, tile), lambda i: (0, i)),
        name="micro_solve",
    )(bundle, stiffness, precond, force, couple, products, coef)


def extend(field):
    return with_halo(field, (("macro", 1), ("micro", 2)), 1)


def cg_kernel(
    sizes,
    load_ref,
    elem_ref,
    inc_ref,
    res_ref,
    residual,
    direction,
    along,
    increment,
    image,
    send_halo,
    halo,
    part,
    got_micro,
    middle,
    got_macro,
    send_sem,
    recv_sem,
    micro_send,
    micro_recv,
    macro_send,
    macro_recv,
):
    count_x, count_y, n_macro, n_micro = sizes
    wide = count_y + 2
    rows, lanes = load_ref.shape[1], load_ref.shape[2]
    a, b = lax.axis_index("macro"), lax.axis_index("micro")

    def inside(dx, dy):
        test = None
        for place, step, count in ((a, dx, n_macro), (b, dy, n_micro)):
            if step != 0:
                good = (place > 0) if step < 0 else (place < count - 1)
                test = good if test is None else jnp.logical_and(test, good)
        return test

    barrier = pltpu.get_barrier_semaphore()
    for step in range(1, n_micro):
        pl.semaphore_signal(
            barrier, inc=1, device_id=(a, lax.rem(b + step, n_micro)), device_id_type=MESH
        )
    for step in range(1, n_macro):
        pl.semaphore_signal(
            barrier, inc=1, device_id=(lax.rem(a + step, n_macro), b), device_id_type=MESH
        )
    corners = [(dx, dy) for dx, dy in AROUND if dx != 0 and dy != 0]
    for dx, dy in corners:
        pl.semaphore_signal(
            barrier,
            inc=1,
            device_id=(lax.rem(a + dx + n_macro, n_macro), lax.rem(b + dy + n_micro, n_micro)),
            device_id_type=MESH,
        )
    pl.semaphore_wait(barrier, n_micro - 1 + n_macro - 1 + len(corners))
    for at, (dx, dy) in enumerate(AROUND):

        @pl.when(jnp.logical_not(inside(dx, dy)))
        def _():
            for it in range(ITERS + 1):
                halo[it, at] = jnp.zeros(halo.shape[2:], jnp.float32)

    def near(step, count):
        return {0: list(range(1, count + 1)), -1: [1], 1: [count]}[step]

    def far(step, count):
        return {0: list(range(1, count + 1)), -1: [0], 1: [count + 1]}[step]

    def places(at, pick):
        dx, dy = AROUND[at]
        return [i * wide + j for i in pick(dx, count_x) for j in pick(dy, count_y)]

    def hop(it, at):
        dx, dy = AROUND[at]
        other = len(AROUND) - 1 - at
        return pltpu.make_async_remote_copy(
            src_ref=send_halo.at[it, at],
            dst_ref=halo.at[it, other],
            send_sem=send_sem.at[it, at],
            recv_sem=recv_sem.at[it, other],
            device_id=(a + dx, b + dy),
            device_id_type=MESH,
        )

    def halo_start(it, ref):
        for at, (dx, dy) in enumerate(AROUND):

            @pl.when(inside(dx, dy))
            def _():
                mine = places(at, near)
                for c in range(3):
                    for k, row in enumerate(mine):
                        send_halo[it, at, pl.ds(c * len(mine) + k, 1)] = ref[c, pl.ds(row, 1)]
                hop(it, at).start()

    def halo_finish(it, ref):
        for at, (dx, dy) in enumerate(AROUND):

            @pl.when(inside(dx, dy))
            def _():
                hop(it, at).wait_send()
                pltpu.make_async_remote_copy(
                    src_ref=send_halo.at[it, at],
                    dst_ref=halo.at[it, at],
                    send_sem=send_sem.at[it, at],
                    recv_sem=recv_sem.at[it, at],
                    device_id=(a + dx, b + dy),
                    device_id_type=MESH,
                ).wait_recv()

        for at in range(len(AROUND)):
            theirs = places(at, far)
            for c in range(3):
                for k, row in enumerate(theirs):
                    ref[c, pl.ds(row, 1)] = halo[it, at, pl.ds(c * len(theirs) + k, 1)]

    row_at = lax.broadcasted_iota(jnp.int32, (rows, lanes), 0)
    lane_at = lax.broadcasted_iota(jnp.int32, (rows, lanes), 1)
    own = row_at < 0
    for i in range(1, count_x + 1):
        low = i * wide + 1
        own = jnp.logical_or(own, jnp.logical_and(row_at >= low, row_at < low + count_y))

    def up(value, axis):
        if axis == 2:
            moved = pltpu.roll(value, lanes - 1, 1)
            return jnp.where(lane_at == lanes - 1, 0.0, moved)
        return pltpu.roll(value, rows - (wide if axis == 0 else 1), 0)

    def down(value, axis):
        if axis == 2:
            return jnp.where(lane_at == 0, 0.0, pltpu.roll(value, 1, 1))
        return pltpu.roll(value, wide if axis == 0 else 1, 0)

    def strain_of(ref):
        grads = []
        for c in range(3):
            value = ref[c]
            moved = up(value, 2)
            total, gap = value + moved, moved - value
            total_up, gap_up = up(total, 1), up(gap, 1)
            flat, slope_y, slope_z = total + total_up, total_up - total, gap + gap_up
            grads.append(
                (
                    0.25 * (up(flat, 0) - flat),
                    0.25 * (up(slope_y, 0) + slope_y),
                    0.25 * (up(slope_z, 0) + slope_z),
                )
            )
        return [
            grads[0][0],
            grads[1][1],
            grads[2][2],
            grads[1][2] + grads[2][1],
            grads[0][2] + grads[2][0],
            grads[0][1] + grads[1][0],
        ]

    def force_of(stress, c):
        first, second, third = (stress[VOIGT[c][d]] for d in range(3))
        first = first + down(first, 2)
        second = second + down(second, 2)
        third = down(third, 2) - third
        first = first + down(first, 1)
        rest = down(second, 1) - second + third + down(third, 1)
        return 0.25 * (down(first, 0) - first + rest + down(rest, 0))

    stress = [elem_ref[i] for i in range(6)]
    for c in range(3):
        residual[c] = jnp.where(own, load_ref[c] - force_of(stress, c), 0.0)
        direction[c] = jnp.zeros((rows, lanes), jnp.float32)
        along[c] = jnp.zeros((rows, lanes), jnp.float32)
        increment[c] = jnp.zeros((rows, lanes), jnp.float32)
    halo_start(ITERS, residual)
    halo_finish(ITERS, residual)

    def gather_start(it, src, dst, count, me, send, recv, device):
        copies = []
        for step in range(1, count):
            copy = pltpu.make_async_remote_copy(
                src_ref=src.at[it],
                dst_ref=dst.at[it, me],
                send_sem=send.at[it, step - 1],
                recv_sem=recv.at[it, step - 1],
                device_id=device(lax.rem(me + step, count)),
                device_id_type=MESH,
            )
            copy.start()
            copies.append(copy)
        dst[it, me] = src[it]
        return copies

    def gather_finish(it, copies, dst, count):
        for copy in copies:
            copy.wait()
        total = dst[it, 0]
        for at in range(1, count):
            total = total + dst[it, at]
        return total

    def step_body(it, carry):
        norm_old, alpha_old = carry
        strain = strain_of(residual)
        stress = []
        for i in range(6):
            value = None
            for j in range(6):
                term = elem_ref[6 + PAIR_AT[(min(i, j), max(i, j))]] * strain[j]
                value = term if value is None else value + term
            stress.append(value)
        norm = jnp.zeros((rows, lanes), jnp.float32)
        cross = jnp.zeros((rows, lanes), jnp.float32)
        for c in range(3):
            here = residual[c]
            new = jnp.where(own, MASS * here + force_of(stress, c), 0.0)
            image[c] = new
            kept = jnp.where(own, here, 0.0)
            norm = norm + kept * kept
            cross = cross + kept * new

        def folded(value):
            value = jnp.sum(value, axis=0, keepdims=True)
            total = value[:, :128]
            for at in range(128, lanes, 128):
                total = total + value[:, at : at + 128]
            return total

        tile_row = lax.broadcasted_iota(jnp.int32, (8, 128), 0)
        part[it] = jnp.where(
            tile_row == 0, folded(norm), jnp.where(tile_row == 1, folded(cross), 0.0)
        )
        copies = gather_start(
            it, part, got_micro, n_micro, b, micro_send, micro_recv, lambda other: (a, other)
        )
        halo_start(it, image)
        middle[it] = gather_finish(it, copies, got_micro, n_micro)
        copies = gather_start(
            it, middle, got_macro, n_macro, a, macro_send, macro_recv, lambda other: (other, b)
        )
        halo_finish(it, image)
        totals = jnp.sum(gather_finish(it, copies, got_macro, n_macro), axis=1, keepdims=True)
        norm_now, product = totals[0:1], totals[1:2]
        first = jnp.full((1, 1), it, jnp.int32) == 0
        ratio = jnp.where(first, 0.0, norm_now / norm_old)
        alpha = norm_now / (product - ratio * norm_now / alpha_old)
        for c in range(3):
            here = residual[c]
            toward = here + ratio * direction[c]
            drop = image[c] + ratio * along[c]
            direction[c] = toward
            along[c] = drop
            increment[c] = increment[c] + alpha * toward
            residual[c] = here - alpha * drop
        return norm_now, alpha

    lax.fori_loop(
        0, ITERS, step_body, (jnp.ones((1, 1), jnp.float32), jnp.ones((1, 1), jnp.float32))
    )
    for c in range(3):
        for i in range(count_x):
            low = (i + 1) * wide + 1
            inc_ref[c, i] = increment[c, pl.ds(low, count_y)]
            res_ref[c, i] = residual[c, pl.ds(low, count_y)]


def conjugate_gradients(load, elements):
    _, count_x, count_y, count_z = load.shape
    n_macro, n_micro = lax.axis_size("macro"), lax.axis_size("micro")
    flat = (count_x + 2) * (count_y + 2)
    rows = -(-flat // 8) * 8

    def laid(value, high):
        value = jnp.pad(value, ((0, 0), (1 - high, 1), (1 - high, 1), (0, 0)))
        value = value.reshape(value.shape[0], flat, count_z)
        return jnp.pad(value, ((0, 0), (0, rows - flat), (0, 0)))

    side = -(-3 * max(count_x, count_y) // 8) * 8
    node = pltpu.VMEM((3, rows, count_z), jnp.float32)
    around = pltpu.VMEM((ITERS + 1, len(AROUND), side, count_z), jnp.float32)
    dma = pltpu.SemaphoreType.DMA

    def body(*refs):
        cg_kernel((count_x, count_y, n_macro, n_micro), *refs)

    vmem = pl.BlockSpec(memory_space=pltpu.VMEM)
    return pl.pallas_call(
        body,
        out_shape=[jax.ShapeDtypeStruct(load.shape, jnp.float32)] * 2,
        in_specs=[vmem, vmem],
        out_specs=[vmem, vmem],
        scratch_shapes=[node] * 5
        + [
            around,
            around,
            pltpu.VMEM((ITERS, 8, 128), jnp.float32),
            pltpu.VMEM((ITERS, n_micro, 8, 128), jnp.float32),
            pltpu.VMEM((ITERS, 8, 128), jnp.float32),
            pltpu.VMEM((ITERS, n_macro, 8, 128), jnp.float32),
            dma((ITERS + 1, len(AROUND))),
            dma((ITERS + 1, len(AROUND))),
            dma((ITERS, n_micro - 1)),
            dma((ITERS, n_micro - 1)),
            dma((ITERS, n_macro - 1)),
            dma((ITERS, n_macro - 1)),
        ],
        compiler_params=pltpu.CompilerParams(collective_id=0, has_side_effects=True),
        name="conjugate_gradients",
    )(laid(load, 0), laid(elements, 1))


def shards(
    displacement,
    load,
    routes,
    counts,
    stiffness,
    precond,
    forcing,
    coupling,
    lame_first,
    lame_shear,
):
    count_x, count_y, count_z = (
        displacement.shape[1],
        displacement.shape[2],
        displacement.shape[3],
    )
    points = count_x * count_y * count_z
    owners = lax.axis_size("micro")
    capacity = max(2, 2 * points // owners)
    strain_ext = element_strain(extend(displacement))
    strain_points = strain_ext[:, 1:, 1:].reshape(6, points)
    owner_of = routes.reshape(points)
    sweeps_of = counts.reshape(points)
    onehot = (owner_of[:, None] == jnp.arange(owners, dtype=jnp.int32)[None, :]).astype(jnp.int32)
    ranks = jnp.sum((jnp.cumsum(onehot, axis=0) - 1) * onehot, axis=1)
    target = owner_of * capacity + ranks
    bundle = jnp.concatenate([strain_points, sweeps_of.astype(jnp.float32)[None]], axis=0)
    bundle = jnp.pad(bundle, ((0, 1), (0, 0)))
    send = jnp.zeros((8, owners * capacity), jnp.float32).at[:, target].set(
        bundle, unique_indices=True, mode="promise_in_bounds"
    )
    got = lax.all_to_all(send, "micro", split_axis=1, concat_axis=1, tiled=True)
    rows = micro_solve(
        got,
        stiffness[0],
        precond[0],
        forcing[0],
        coupling[0],
        lame_first[0],
        lame_shear[0],
        PAIRS,
    )
    back = lax.all_to_all(rows, "micro", split_axis=1, concat_axis=1, tiled=True)
    values = jnp.take(back, target, axis=1, unique_indices=True, mode="clip")
    values = values.reshape(back.shape[0], count_x, count_y, count_z)
    left_x = passed_along(values[:, -1:], "macro", 1)
    values = jnp.concatenate([left_x, values], axis=1)
    left_y = passed_along(values[:, :, -1:], "micro", 1)
    values = jnp.concatenate([left_y, values], axis=2)
    return tuple(conjugate_gradients(load, values))


def solution(mesh):
    in_specs = (
        P(None, "macro", "micro", None),
        P(None, "macro", "micro", None),
        P("macro", "micro", None, None),
        P("macro", "micro", None),
        P("micro", None, None),
        P("micro", None, None),
        P("micro", None, None),
        P("micro", None, None),
        P("micro"),
        P("micro"),
    )
    out_specs = (P(None, "macro", "micro", None), P(None, "macro", "micro", None))
    return jax.shard_map(shards, mesh=mesh, in_specs=in_specs, out_specs=out_specs, check_vma=False)
```
